512 devices in a mesh: leaf: 32 (over z, x), slab: 16 (over y, core).
Axes of the slice: x: 4, y: 8, z: 8, core: 2. Of those that a mesh axis runs over, the one named last changes fastest.
Arguments:
- leaf_basis: bfloat16 [16, 256, 512, 128], P('slab', 'leaf'), may hold values from -0.25 to 0.25
- point_counts: int32 [16, 256], P('slab', 'leaf'), may hold values from 256 to 512, as said below
- leaf_transfer: float32 [16, 256, 128, 128], P('slab', 'leaf')
- node_transfer: float32 [16, 32, 128, 128], P('slab', 'leaf')
- group_transfer: float32 [16, 4, 128, 128], P('slab')
- positions: float32 [16, 256, 3, 512], P('slab', 'leaf'), may hold values from 0 to 2
- moments: float32 [16, 256, 512], P('slab', 'leaf'), may hold values from -6 to 6
- send_tiles: int32 [16, 128], P('slab', 'leaf'), may hold values from 0 to 7, as said below
- neighbours: int32 [16, 256, 4], P('slab', 'leaf'), may hold values from 0 to 11
Outputs:
- leaf_factors: float32 [16, 256, 128, 128], P('slab', 'leaf')
- node_factors: float32 [16, 32, 128, 128], P('slab', 'leaf')
- group_factors: float32 [16, 32, 128, 128], P('slab', 'leaf')
- root_factors: float32 [16, 32, 128, 128], P('slab', 'leaf')
- near_field: float32 [16, 256, 512], P('slab', 'leaf')
The draws below stay inside these ranges and needn't reach their ends.
Inputs may be any that keep to these rules, and one draw needn't show every extreme that they name: `point_counts`: in each first-level node one leaf has all 512 slots live. `send_tiles`: within each node, the 2 lower-face and 2 upper-face entries name 4 different leaves of that node, numbered 0 to 7. `neighbours`: numbers below 8 are the node's own leaves; the next 2 are the faces received from the slab below, the last 2 those from the slab above.
All inputs are finite; a program needn't handle non-finite values.
Results may differ from the reference program's by a relative error of at most 0.0003.
Values sent between devices are 32-bit elements; how exact they have to be, the bound alone decides.
A program may use at most 64 MiB of HBM per device.

```python
import math
import jax
import jax.numpy as jnp
from jax import lax

RANK = 128
PTS = 512
CHILDREN = 8
NB = 4
HALO = 2
SLABS = 16
NODES = 32
TREE_LEAVES = 256
GROUPS = 4


def transfer_draw(key, shape):
    noise = jax.random.normal(key, shape, jnp.float32)
    rows = lax.broadcasted_iota(jnp.int32, shape, len(shape) - 2)
    columns = lax.broadcasted_iota(jnp.int32, shape, len(shape) - 1)
    identity = (rows == columns).astype(jnp.float32)
    return (identity + 0.3 * noise / math.sqrt(RANK)) / math.sqrt(CHILDREN)


def draw_leaf_transfer(key, part):
    return transfer_draw(key, (SLABS, TREE_LEAVES, RANK, RANK))


def draw_node_transfer(key, part):
    return transfer_draw(key, (SLABS, NODES, RANK, RANK))


def draw_group_transfer(key, part):
    return transfer_draw(key, (SLABS, GROUPS, RANK, RANK))


def draw_point_counts(key, part):
    first, second = jax.random.split(key)
    counts = jax.random.randint(first, (SLABS, TREE_LEAVES), PTS // 2, PTS + 1)
    chosen = jax.random.randint(second, (SLABS, NODES, 1), 0, CHILDREN)
    filled = lax.broadcasted_iota(jnp.int32, (SLABS, NODES, CHILDREN), 2) == chosen
    return jnp.where(filled.reshape(SLABS, TREE_LEAVES), PTS, counts).astype(jnp.int32)


def draw_send_tiles(key, part):
    shape = (SLABS, NODES, CHILDREN)
    scores = jax.random.randint(key, shape, 0, 1048576) * CHILDREN + lax.broadcasted_iota(jnp.int32, shape, 2)
    order = jnp.argsort(scores, axis=2, stable=True).astype(jnp.int32)
    return order[:, :, :2 * HALO].reshape(SLABS, NODES * 2 * HALO)


def plant(drawn, stream_key, least, high):
    longest = drawn.shape.index(max(drawn.shape))
    spots = []
    for shift in (0, 1):
        where = [jax.random.randint(jax.random.fold_in(stream_key, axis), (), 0, length) for axis, length in enumerate(drawn.shape)]
        where[longest] = (where[longest] + shift) % drawn.shape[longest]
        spots.append(tuple(where))
    return drawn.at[spots[0]].set(least).at[spots[1]].set(high)


def block_levels(rng, shape, cuts, low, top_value):
    level = 1.0
    for axis_at, parts in cuts:
        heights = jax.random.uniform(jax.random.fold_in(jax.random.fold_in(rng, 6), axis_at), (parts,), jnp.float32, low / len(cuts), top_value / len(cuts))
        level = level * jnp.repeat(jnp.exp(heights), shape[axis_at] // parts).reshape((-1,) + (1,) * (len(shape) - 1 - axis_at))
    return level


def gaussian(own_key, extent, width, most, shards=(), kind=jnp.bfloat16):
    drawn = width * jax.random.normal(own_key, extent, jnp.float32)
    if shards:
        drawn = drawn * block_levels(own_key, extent, shards, -0.22, 0.18)
    return jnp.clip(drawn, -most, most).astype(kind)


def setup_inputs(seed: int = 0) -> dict:
    arg_keys = jax.random.split(jax.random.key(seed), 10)
    return {
        "leaf_basis": gaussian(arg_keys[0], (SLABS, TREE_LEAVES, PTS, RANK), PTS ** -0.5, 0.25, ((0, 16), (1, 32))),
        "point_counts": draw_point_counts(jax.random.fold_in(arg_keys[9], 71), 0),
        "leaf_transfer": draw_leaf_transfer(jax.random.fold_in(arg_keys[9], 71), 0),
        "node_transfer": draw_node_transfer(jax.random.fold_in(arg_keys[9], 71), 0),
        "group_transfer": draw_group_transfer(jax.random.fold_in(arg_keys[9], 71), 0),
        "positions": jnp.clip(2.0 * jax.random.uniform(arg_keys[5], (SLABS, TREE_LEAVES, 3, PTS), jnp.float32) ** block_levels(arg_keys[5], (SLABS, TREE_LEAVES, 3, PTS), ((0, 16), (1, 32)), -0.2, 0.2), 0.0, 2.0),
        "moments": gaussian(arg_keys[6], (SLABS, TREE_LEAVES, PTS), 1.0, 6.0, ((0, 16), (1, 32)), jnp.float32),
        "send_tiles": draw_send_tiles(jax.random.fold_in(arg_keys[9], 71), 0),
        "neighbours": plant(jax.random.randint(arg_keys[8], (SLABS, TREE_LEAVES, NB), 0, CHILDREN + 2 * HALO), jax.random.fold_in(arg_keys[8], 1), 0, (CHILDREN + 2 * HALO) - 1).astype(jnp.int32),
    }


soften = 0.25
coupling = 0.03
highest = lax.Precision.HIGHEST

def congruent(transfer, gram):
    inner = jnp.matmul(gram, transfer, precision=highest)
    return jnp.matmul(jnp.swapaxes(transfer, -1, -2), inner, precision=highest)

def near_tile(targets, sources):
    first_gap = targets[0][:, None, None] - sources[None, :, 0, :]
    second_gap = targets[1][:, None, None] - sources[None, :, 1, :]
    third_gap = targets[2][:, None, None] - sources[None, :, 2, :]
    radius = first_gap * first_gap + second_gap * second_gap + third_gap * third_gap + soften
    kernel = (radius - 3.0 * third_gap * third_gap) * radius ** (-2.5)
    return coupling * jnp.sum(kernel * sources[None, :, 3, :], axis=(1, 2))

def leaf_gram(block):
    wide = block.astype(jnp.float32)
    return jnp.einsum('lpr,lps->lrs', wide, wide)

def reference(leaf_basis, point_counts, leaf_transfer, node_transfer, group_transfer, positions, moments, send_tiles, neighbours):
    live = lax.broadcasted_iota(jnp.int32, (SLABS, TREE_LEAVES, PTS), 2) < point_counts[:, :, None]
    masked = jnp.where(live[..., None], leaf_basis, jnp.zeros((), jnp.bfloat16))
    grams = lax.map(leaf_gram, masked)
    leaf_factors = jnp.linalg.cholesky(grams)
    node_grams = congruent(leaf_transfer, grams).reshape(SLABS, NODES, CHILDREN, RANK, RANK).sum(2)
    node_factors = jnp.linalg.cholesky(node_grams)
    group_grams = congruent(node_transfer, node_grams).reshape(SLABS, GROUPS, CHILDREN, RANK, RANK).sum(2)
    group_factors = jnp.repeat(jnp.linalg.cholesky(group_grams), CHILDREN, axis=1)
    root_single = jnp.linalg.cholesky(congruent(group_transfer, group_grams).sum(1))
    root_factors = jnp.broadcast_to(root_single[:, None], (SLABS, NODES, RANK, RANK))
    charged = moments * live.astype(jnp.float32)
    sources = jnp.concatenate([positions, charged[:, :, None, :]], axis=2).reshape(SLABS, NODES, CHILDREN, 4, PTS)
    tiles = send_tiles.reshape(SLABS, NODES, 2 * HALO)
    faces = jax.vmap(jax.vmap(lambda block, picks: block[picks]))(sources, tiles)
    empty = jnp.zeros((1, NODES, HALO, 4, PTS), jnp.float32)
    below = jnp.concatenate([empty, faces[:-1, :, HALO:]], axis=0)
    above = jnp.concatenate([faces[1:, :, :HALO], empty], axis=0)
    extended = jnp.concatenate([sources, below, above], axis=2)
    links = neighbours.reshape(SLABS * NODES, CHILDREN, NB)
    targets = positions.reshape(SLABS * NODES, CHILDREN, 3, PTS)

    def node_field(item):
        block, link, target = item
        picked = block[link]
        return lax.map(lambda pair: near_tile(pair[0], pair[1]), (target, picked))
    field = lax.map(node_field, (extended.reshape(SLABS * NODES, CHILDREN + 2 * HALO, 4, PTS), links, targets))
    near_field = jnp.where(live, field.reshape(SLABS, TREE_LEAVES, PTS), jnp.zeros((), jnp.float32))
    return (leaf_factors, node_factors, group_factors, root_factors, near_field)
```

```python
import functools

import jax
import jax.numpy as jnp
from jax import lax
from jax.experimental import pallas as pl
from jax.experimental.pallas import tpu as pltpu
from jax.sharding import PartitionSpec as P

RANK = 128
PTS = 512
CHILDREN = 8
NB = 4
ROWS = 16
SPLIT = 48
MESH = pltpu.MESH if hasattr(pltpu, "MESH") else pl.DeviceIdType.MESH

f32 = jnp.float32
bf16 = jnp.bfloat16
highest = lax.Precision.HIGHEST
over_rows = (((0,), (0,)), ((), ()))


def split3(x):
    high = x.astype(bf16)
    rest = x - high.astype(f32)
    middle = rest.astype(bf16)
    return high, middle, (rest - middle.astype(f32)).astype(bf16)


def factor_panel(grams, uppers, mats, k, size):
    groups = size // 8
    sub = lax.broadcasted_iota(jnp.int32, (8, RANK), 0)
    lane = lax.broadcasted_iota(jnp.int32, (8, RANK), 1)
    start = pl.multiple_of(k * size, size)
    count = len(mats)

    def spread(x, s):
        return jnp.broadcast_to(x[s : s + 1, :], (8, RANK))

    rows = [[grams[m, pl.ds(pl.multiple_of(start + 8 * g, 8), 8), :] for g in range(groups)] for m in mats]
    columns = [
        [
            [
                jnp.take_along_axis(rows[i][g], jnp.full((8, RANK), start + j, jnp.int32), axis=1)
                if g >= j // 8
                else None
                for g in range(groups)
            ]
            for j in range(size)
        ]
        for i in range(count)
    ]
    upper = [[None] * groups for _ in mats]
    for r in range(size):
        gr, sr = divmod(r, 8)
        for i in range(count):
            pivot = spread(columns[i][r][gr], sr)
            inverse = 1.0 / pivot
            row = spread(rows[i][gr], sr)
            scaled = row * lax.rsqrt(pivot)
            upper[i][gr] = scaled if sr == 0 else jnp.where(sub >= sr, scaled, upper[i][gr])
            weights = {}
            for g in range(gr, groups):
                if g == gr and sr == 7:
                    continue
                weight = columns[i][r][g] * inverse
                weights[g] = jnp.where(sub > sr, weight, 0.0) if g == gr else weight
            for j in range(r + 1, size):
                entry = spread(columns[i][r][j // 8], j % 8)
                for g in range(max(gr, j // 8), groups):
                    if g in weights:
                        columns[i][j][g] = columns[i][j][g] - weights[g] * entry
            for g in weights:
                rows[i][g] = rows[i][g] - weights[g] * row
    for i, m in enumerate(mats):
        kept = [jnp.where(lane >= sub + (start + 8 * g), upper[i][g], 0.0) for g in range(groups)]
        panel = jnp.concatenate(kept, axis=0) if groups > 1 else kept[0]
        uppers[m, pl.ds(start, size), :] = panel
        high, middle, low = split3(panel)
        left = jnp.concatenate([high, high, high, middle, middle, low], axis=0)
        right = jnp.concatenate([high, middle, low, high, middle, high], axis=0)
        grams[m] = grams[m] - lax.dot_general(left, right, over_rows, preferred_element_type=f32)


def stacked(values):
    rows = lax.broadcasted_iota(jnp.int32, (8, PTS), 0)
    out = jnp.zeros((8, PTS), f32)
    for i, value in enumerate(values):
        out = jnp.where(rows == i, jnp.broadcast_to(value, (8, PTS)), out)
    return out


def source_features(x, y, z, q):
    x, y, z = x - 1.0, y - 1.0, z - 1.0
    flat, high2 = x * x + y * y, z * z
    one, none = jnp.ones_like(x), jnp.zeros_like(x)
    first = stacked([-2.0 * x, -2.0 * y, -2.0 * z, one, none, flat + high2 + 0.25])
    second = stacked([-2.0 * x * q, -2.0 * y * q, 4.0 * z * q, none, q, q * (flat - 2.0 * high2 + 0.25)])
    out = []
    for form in (first, second):
        high, middle, low = [piece.astype(f32) for piece in split3(form)]
        out += [high, middle, low, high, middle, high]
    return jnp.concatenate(out, axis=0)


def target_features(x, y, z):
    x, y, z = x - 1.0, y - 1.0, z - 1.0
    flat, high2 = x * x + y * y, z * z
    form = stacked([x, y, z, flat + high2, flat - 2.0 * high2, jnp.ones_like(x)])
    high, middle, low = [piece.astype(f32) for piece in split3(form)]
    return jnp.concatenate([high, high, high, middle, middle, low], axis=0).astype(bf16)


def field_of(targets, features, picks, width=256, depth=64):
    none = jnp.zeros((SPLIT, width), bf16)
    out = []
    for j in range(PTS // width):
        form = targets[:, j * width : (j + 1) * width]
        for_radius = jnp.concatenate([form, none], axis=0)
        for_weight = jnp.concatenate([none, form], axis=0)
        total = jnp.zeros((8, width), f32)
        for pick in picks:
            for c in range(PTS // depth):
                block = features[pick, c * depth : (c + 1) * depth, :]
                radius = jnp.dot(block, for_radius, preferred_element_type=f32)
                weight = jnp.dot(block, for_weight, preferred_element_type=f32)
                root = lax.rsqrt(radius)
                square = root * root
                value = (weight * root) * (square * square)
                total = total + jnp.sum(value.reshape(depth // 8, 8, width), axis=0)
        out.append(total)
    return jnp.concatenate(out, axis=1)


def kernel(
    slabs,
    spans,
    basis,
    leaf_transfer,
    node_transfer,
    group_transfer,
    positions,
    moments,
    counts,
    tiles,
    neighbours,
    leaf_out,
    node_out,
    group_out,
    root_out,
    near_out,
    own,
    faces,
    halo,
    features,
    grams,
    uppers,
    lifted,
    landed,
    summed,
    crossed,
    rooted,
    reduced,
    reduced_upper,
    face_send,
    face_recv,
    one_send,
    one_recv,
    two_send,
    two_recv,
    cross_send,
    cross_recv,
    three_send,
    three_recv,
):
    leaf = lax.axis_index("leaf")
    slab = lax.axis_index("slab")
    member, group = leaf % CHILDREN, leaf // CHILDREN
    peers = [group * CHILDREN + (member + d) % CHILDREN for d in range(1, CHILDREN)]
    kin = [((group + d) % spans) * CHILDREN + member for d in range(1, spans)]
    above, below = (slab + 1) % slabs, (slab + slabs - 1) % slabs
    barrier = pltpu.get_barrier_semaphore()
    for other in peers + kin:
        pl.semaphore_signal(barrier, inc=1, device_id={"leaf": other}, device_id_type=MESH)
    for other in (above, below):
        pl.semaphore_signal(barrier, inc=1, device_id={"slab": other}, device_id_type=MESH)

    points = lax.broadcasted_iota(jnp.int32, (1, PTS), 1)
    for l in range(CHILDREN):
        for axis in range(3):
            own[l, axis : axis + 1, :] = positions[axis, l : l + 1, :]
        own[l, 3:4, :] = moments[l : l + 1, :] * (points < counts[0, l]).astype(f32)
    for f in range(4):
        faces[f] = own[tiles[0, f]]

    slots = lax.broadcasted_iota(jnp.int32, (PTS, RANK), 0)
    inner = []
    for l in range(CHILDREN):
        live = jnp.where(slots < counts[0, l], basis[l].astype(f32), 0.0).astype(bf16)
        gram = lax.dot_general(live, live, over_rows, preferred_element_type=f32)
        grams[l] = gram
        inner.append(jnp.dot(gram, leaf_transfer[l], precision=highest, preferred_element_type=f32))
    every = leaf_transfer[...].reshape(CHILDREN * RANK, RANK)
    node = lax.dot_general(every, jnp.concatenate(inner, axis=0), over_rows, precision=highest, preferred_element_type=f32)
    grams[CHILDREN] = node

    def congruent(transfer, gram):
        product = jnp.dot(gram, transfer, precision=highest, preferred_element_type=f32)
        return lax.dot_general(transfer, product, over_rows, precision=highest, preferred_element_type=f32)

    to_group = congruent(node_transfer[...], node)
    to_root = congruent(group_transfer[group], to_group)
    for c in range(CHILDREN):
        lifted[c, 0] = to_group[c * ROWS : (c + 1) * ROWS, :]
        lifted[c, 1] = to_root[c * ROWS : (c + 1) * ROWS, :]

    pl.semaphore_wait(barrier, len(peers) + len(kin) + 2)

    def remote(source, target, send, recv, where):
        return pltpu.make_async_remote_copy(
            src_ref=source, dst_ref=target, send_sem=send, recv_sem=recv, device_id=where, device_id_type=MESH
        )

    up = remote(faces.at[pl.ds(2, 2)], halo.at[pl.ds(0, 2)], face_send.at[0], face_recv.at[0], {"slab": above})
    down = remote(faces.at[pl.ds(0, 2)], halo.at[pl.ds(2, 2)], face_send.at[1], face_recv.at[1], {"slab": below})
    firsts = [
        remote(
            lifted.at[(member + d) % CHILDREN],
            landed.at[d - 1],
            one_send.at[d - 1],
            one_recv.at[d - 1],
            {"leaf": peers[d - 1]},
        )
        for d in range(1, CHILDREN)
    ]
    for copy in firsts:
        copy.start()
    up.start()
    down.start()

    def own_features(l, carry):
        s = own[l]
        features[l] = source_features(s[0:1], s[1:2], s[2:3], s[3:4]).T.astype(bf16)
        return carry

    lax.fori_loop(0, CHILDREN, own_features, 0)

    def first_panels(k, carry):
        factor_panel(grams, uppers, range(CHILDREN + 1), k, 8)
        return carry

    def second_panels(k, carry):
        factor_panel(reduced, reduced_upper, range(2), k, 16)
        return carry

    def near(l, carry):
        s = own[l]
        total = field_of(
            target_features(s[0:1], s[1:2], s[2:3]), features, [neighbours[k, l] for k in range(NB)]
        )
        near_out[pl.ds(l, 1), :] = jnp.where(
            points < counts[0, l], 0.03 * jnp.sum(total, axis=0, keepdims=True), 0.0
        )
        return carry

    lax.fori_loop(0, RANK // 8, first_panels, 0)

    for copy in firsts:
        copy.wait()
    total = lifted[member]
    for d in range(1, CHILDREN):
        total = total + landed[d - 1]
    summed[...] = total
    mine = pl.ds(pl.multiple_of(member * ROWS, ROWS), ROWS)
    reduced[0, mine, :] = total[0]
    seconds = [
        remote(
            summed.at[0], reduced.at[0, mine], two_send.at[d - 1], two_recv.at[d - 1], {"leaf": peers[d - 1]}
        )
        for d in range(1, CHILDREN)
    ]
    crosses = [
        remote(summed.at[1], crossed.at[d - 1], cross_send.at[d - 1], cross_recv.at[d - 1], {"leaf": kin[d - 1]})
        for d in range(1, spans)
    ]
    for copy in crosses + seconds:
        copy.start()

    up.wait()
    down.wait()

    def halo_features(e, carry):
        s = halo[e]
        there = jnp.where(e < 2, slab > 0, slab < slabs - 1).astype(f32)
        features[CHILDREN + e] = source_features(s[0:1], s[1:2], s[2:3], s[3:4] * there).T.astype(bf16)
        return carry

    lax.fori_loop(0, 4, halo_features, 0)
    lax.fori_loop(0, 3, near, 0)

    for copy in crosses:
        copy.wait()
    total = summed[1]
    for d in range(1, spans):
        total = total + crossed[d - 1]
    rooted[...] = total
    reduced[1, mine, :] = total
    thirds = [
        remote(rooted, reduced.at[1, mine], three_send.at[d - 1], three_recv.at[d - 1], {"leaf": peers[d - 1]})
        for d in range(1, CHILDREN)
    ]
    for copy in thirds:
        copy.start()
    lax.fori_loop(3, CHILDREN, near, 0)
    for copy in seconds + thirds:
        copy.wait()
    lax.fori_loop(0, RANK // 16, second_panels, 0)
    for l in range(CHILDREN):
        leaf_out[l] = uppers[l].T
    node_out[...] = uppers[CHILDREN].T
    group_out[...] = reduced_upper[0].T
    root_out[...] = reduced_upper[1].T


def body(
    leaf_basis,
    point_counts,
    leaf_transfer,
    node_transfer,
    group_transfer,
    positions,
    moments,
    send_tiles,
    neighbours,
):
    spans = lax.axis_size("leaf") // CHILDREN
    slabs = lax.axis_size("slab")
    vmem = pl.BlockSpec(memory_space=pltpu.VMEM)
    smem = pl.BlockSpec(memory_space=pltpu.SMEM)
    square = jax.ShapeDtypeStruct((RANK, RANK), f32)
    dma = pltpu.SemaphoreType.DMA
    leaf, node, group, root, near = pl.pallas_call(
        functools.partial(kernel, slabs, spans),
        out_shape=(
            jax.ShapeDtypeStruct((CHILDREN, RANK, RANK), f32),
            square,
            square,
            square,
            jax.ShapeDtypeStruct((CHILDREN, PTS), f32),
        ),
        in_specs=[vmem] * 6 + [smem] * 3,
        out_specs=(vmem,) * 5,
        scratch_shapes=[
            pltpu.VMEM((CHILDREN, 4, PTS), f32),
            pltpu.VMEM((4, 4, PTS), f32),
            pltpu.VMEM((4, 4, PTS), f32),
            pltpu.VMEM((CHILDREN + 4, PTS, 2 * SPLIT), bf16),
            pltpu.VMEM((CHILDREN + 1, RANK, RANK), f32),
            pltpu.VMEM((CHILDREN + 1, RANK, RANK), f32),
            pltpu.VMEM((CHILDREN, 2, ROWS, RANK), f32),
            pltpu.VMEM((CHILDREN - 1, 2, ROWS, RANK), f32),
            pltpu.VMEM((2, ROWS, RANK), f32),
            pltpu.VMEM((spans - 1, ROWS, RANK), f32),
            pltpu.VMEM((ROWS, RANK), f32),
            pltpu.VMEM((2, RANK, RANK), f32),
            pltpu.VMEM((2, RANK, RANK), f32),
            dma((2,)),
            dma((2,)),
            dma((CHILDREN - 1,)),
            dma((CHILDREN - 1,)),
            dma((CHILDREN - 1,)),
            dma((CHILDREN - 1,)),
            dma((spans - 1,)),
            dma((spans - 1,)),
            dma((CHILDREN - 1,)),
            dma((CHILDREN - 1,)),
        ],
        compiler_params=pltpu.CompilerParams(collective_id=0, has_side_effects=True),
        name="upsweep",
    )(
        leaf_basis[0],
        leaf_transfer[0],
        node_transfer[0, 0],
        group_transfer[0],
        jnp.transpose(positions[0], (1, 0, 2)),
        moments[0],
        point_counts,
        send_tiles,
        jnp.transpose(neighbours[0]),
    )
    return leaf[None], node[None, None], group[None, None], root[None, None], near[None]


def solution(mesh):
    in_specs = (
        P("slab", "leaf", None, None),
        P("slab", "leaf"),
        P("slab", "leaf", None, None),
        P("slab", "leaf", None, None),
        P("slab", None, None, None),
        P("slab", "leaf", None, None),
        P("slab", "leaf", None),
        P("slab", "leaf"),
        P("slab", "leaf", None),
    )
    out_specs = (
        P("slab", "leaf", None, None),
        P("slab", "leaf", None, None),
        P("slab", "leaf", None, None),
        P("slab", "leaf", None, None),
        P("slab", "leaf", None),
    )
    return jax.shard_map(body, mesh=mesh, in_specs=in_specs, out_specs=out_specs, check_vma=False)
```

```python
import functools

import jax
import jax.numpy as jnp
from jax import lax
from jax.experimental import pallas as pl
from jax.experimental.pallas import tpu as pltpu
from jax.sharding import PartitionSpec as P

RANK = 128
PTS = 512
CHILDREN = 8
NB = 4
ROWS = 16
EARLY = 3
SPLIT = 48
MESH = pltpu.MESH if hasattr(pltpu, "MESH") else pl.DeviceIdType.MESH

f32 = jnp.float32
bf16 = jnp.bfloat16
highest = lax.Precision.HIGHEST
over_rows = (((0,), (0,)), ((), ()))


def split3(x):
    high = x.astype(bf16)
    rest = x - high.astype(f32)
    middle = rest.astype(bf16)
    return high, middle, (rest - middle.astype(f32)).astype(bf16)


def factor_panel(grams, uppers, mats, k, size):
    groups = size // 8
    sub = lax.broadcasted_iota(jnp.int32, (8, RANK), 0)
    lane = lax.broadcasted_iota(jnp.int32, (8, RANK), 1)
    start = pl.multiple_of(k * size, size)
    count = len(mats)

    def spread(x, s):
        return jnp.broadcast_to(x[s : s + 1, :], (8, RANK))

    rows = [[grams[m, pl.ds(pl.multiple_of(start + 8 * g, 8), 8), :] for g in range(groups)] for m in mats]
    columns = [
        [
            [
                jnp.take_along_axis(rows[i][g], jnp.full((8, RANK), start + j, jnp.int32), axis=1)
                if g >= j // 8
                else None
                for g in range(groups)
            ]
            for j in range(size)
        ]
        for i in range(count)
    ]
    upper = [[None] * groups for _ in mats]
    for r in range(size):
        gr, sr = divmod(r, 8)
        for i in range(count):
            pivot = spread(columns[i][r][gr], sr)
            inverse = 1.0 / pivot
            row = spread(rows[i][gr], sr)
            scaled = row * lax.rsqrt(pivot)
            upper[i][gr] = scaled if sr == 0 else jnp.where(sub >= sr, scaled, upper[i][gr])
            weights = {}
            for g in range(gr, groups):
                if g == gr and sr == 7:
                    continue
                weight = columns[i][r][g] * inverse
                weights[g] = jnp.where(sub > sr, weight, 0.0) if g == gr else weight
            for j in range(r + 1, size):
                entry = spread(columns[i][r][j // 8], j % 8)
                for g in range(max(gr, j // 8), groups):
                    if g in weights:
                        columns[i][j][g] = columns[i][j][g] - weights[g] * entry
            for g in weights:
                rows[i][g] = rows[i][g] - weights[g] * row
    for i, m in enumerate(mats):
        kept = [jnp.where(lane >= sub + (start + 8 * g), upper[i][g], 0.0) for g in range(groups)]
        panel = jnp.concatenate(kept, axis=0) if groups > 1 else kept[0]
        uppers[m, pl.ds(start, size), :] = panel
        high, middle, low = split3(panel)
        left = jnp.concatenate([high, high, high, middle, middle, low], axis=0)
        right = jnp.concatenate([high, middle, low, high, middle, high], axis=0)
        grams[m] = grams[m] - lax.dot_general(left, right, over_rows, preferred_element_type=f32)


def stacked(values):
    rows = lax.broadcasted_iota(jnp.int32, (8, PTS), 0)
    out = jnp.zeros((8, PTS), f32)
    for i, value in enumerate(values):
        out = jnp.where(rows == i, jnp.broadcast_to(value, (8, PTS)), out)
    return out


def source_features(x, y, z, q):
    x, y, z = x - 1.0, y - 1.0, z - 1.0
    flat, high2 = x * x + y * y, z * z
    one, none = jnp.ones_like(x), jnp.zeros_like(x)
    first = stacked([-2.0 * x, -2.0 * y, -2.0 * z, one, none, flat + high2 + 0.25])
    second = stacked([-2.0 * x * q, -2.0 * y * q, 4.0 * z * q, none, q, q * (flat - 2.0 * high2 + 0.25)])
    out = []
    for form in (first, second):
        high, middle, low = [piece.astype(f32) for piece in split3(form)]
        out += [high, middle, low, high, middle, high]
    return jnp.concatenate(out, axis=0)


def target_features(x, y, z):
    x, y, z = x - 1.0, y - 1.0, z - 1.0
    flat, high2 = x * x + y * y, z * z
    form = stacked([x, y, z, flat + high2, flat - 2.0 * high2, jnp.ones_like(x)])
    high, middle, low = [piece.astype(f32) for piece in split3(form)]
    return jnp.concatenate([high, high, high, middle, middle, low], axis=0).astype(bf16)


def field_of(targets, features, picks, width=256, depth=64):
    none = jnp.zeros((SPLIT, width), bf16)
    out = []
    for j in range(PTS // width):
        form = targets[:, j * width : (j + 1) * width]
        for_radius = jnp.concatenate([form, none], axis=0)
        for_weight = jnp.concatenate([none, form], axis=0)
        total = jnp.zeros((8, width), f32)
        for pick in picks:
            for c in range(PTS // depth):
                block = features[pick, c * depth : (c + 1) * depth, :]
                radius = jnp.dot(block, for_radius, preferred_element_type=f32)
                weight = jnp.dot(block, for_weight, preferred_element_type=f32)
                root = lax.rsqrt(radius)
                square = root * root
                value = (weight * root) * (square * square)
                total = total + jnp.sum(value.reshape(depth // 8, 8, width), axis=0)
        out.append(total)
    return jnp.concatenate(out, axis=1)


def kernel(
    slabs,
    nodes,
    basis,
    leaf_transfer,
    node_transfer,
    group_transfer,
    positions,
    moments,
    counts,
    tiles,
    neighbours,
    uppers,
    reduced,
    partial,
    features,
    own,
    faces,
    halo,
    grams,
    lifted,
    landed,
    summed,
    rising,
    risen,
    rooted,
    gathered,
    joined,
    face_send,
    face_recv,
    one_send,
    one_recv,
    two_send,
    two_recv,
    rise_send,
    rise_recv,
    root_send,
    root_recv,
):
    leaf = lax.axis_index("leaf")
    slab = lax.axis_index("slab")
    member, group = leaf % CHILDREN, leaf // CHILDREN
    peers = [group * CHILDREN + (member + d) % CHILDREN for d in range(1, CHILDREN)]
    others = [(leaf + d) % nodes for d in range(1, nodes)]
    above, below = (slab + 1) % slabs, (slab + slabs - 1) % slabs
    barrier = pltpu.get_barrier_semaphore()
    for other in others:
        pl.semaphore_signal(barrier, inc=1, device_id={"leaf": other}, device_id_type=MESH)
    for other in (above, below):
        pl.semaphore_signal(barrier, inc=1, device_id={"slab": other}, device_id_type=MESH)

    points = lax.broadcasted_iota(jnp.int32, (1, PTS), 1)
    for l in range(CHILDREN):
        for axis in range(3):
            own[l, axis : axis + 1, :] = positions[axis, l : l + 1, :]
        own[l, 3:4, :] = moments[l : l + 1, :] * (points < counts[0, l]).astype(f32)
    for f in range(4):
        faces[f] = own[tiles[0, f]]

    slots = lax.broadcasted_iota(jnp.int32, (PTS, RANK), 0)
    inner = []
    for l in range(CHILDREN):
        live = jnp.where(slots < counts[0, l], basis[l].astype(f32), 0.0).astype(bf16)
        gram = lax.dot_general(live, live, over_rows, preferred_element_type=f32)
        grams[l] = gram
        inner.append(jnp.dot(gram, leaf_transfer[l], precision=highest, preferred_element_type=f32))
    every = leaf_transfer[...].reshape(CHILDREN * RANK, RANK)
    node = lax.dot_general(every, jnp.concatenate(inner, axis=0), over_rows, precision=highest, preferred_element_type=f32)
    grams[CHILDREN] = node

    def congruent(transfer, gram):
        product = jnp.dot(gram, transfer, precision=highest, preferred_element_type=f32)
        return lax.dot_general(transfer, product, over_rows, precision=highest, preferred_element_type=f32)

    to_group = congruent(node_transfer[...], node)
    to_root = congruent(group_transfer[group], to_group)
    part = RANK // nodes
    for c in range(CHILDREN):
        lifted[c] = to_group[c * ROWS : (c + 1) * ROWS, :]
    for c in range(nodes):
        rising[c] = to_root[c * part : (c + 1) * part, :]

    pl.semaphore_wait(barrier, len(others) + 2)

    def remote(source, target, send, recv, where):
        return pltpu.make_async_remote_copy(
            src_ref=source, dst_ref=target, send_sem=send, recv_sem=recv, device_id=where, device_id_type=MESH
        )

    up = remote(faces.at[pl.ds(2, 2)], halo.at[pl.ds(0, 2)], face_send.at[0], face_recv.at[0], {"slab": above})
    down = remote(faces.at[pl.ds(0, 2)], halo.at[pl.ds(2, 2)], face_send.at[1], face_recv.at[1], {"slab": below})
    up.start()
    down.start()
    firsts = [
        remote(
            lifted.at[(member + d) % CHILDREN],
            landed.at[d - 1],
            one_send.at[d - 1],
            one_recv.at[d - 1],
            {"leaf": peers[d - 1]},
        )
        for d in range(1, CHILDREN)
    ] + [
        remote(
            rising.at[(leaf + d) % nodes],
            risen.at[d - 1],
            rise_send.at[d - 1],
            rise_recv.at[d - 1],
            {"leaf": others[d - 1]},
        )
        for d in range(1, nodes)
    ]
    for copy in firsts:
        copy.start()

    def own_features(l, carry):
        s = own[l]
        features[l] = source_features(s[0:1], s[1:2], s[2:3], s[3:4]).T.astype(bf16)
        return carry

    lax.fori_loop(0, CHILDREN, own_features, 0)

    def panels(k, carry):
        factor_panel(grams, uppers, range(CHILDREN + 1), k, 8)
        return carry

    def near(l, carry):
        s = own[l]
        partial[l] = field_of(
            target_features(s[0:1], s[1:2], s[2:3]), features, [neighbours[k, l] for k in range(EARLY)]
        )
        return carry

    lax.fori_loop(0, RANK // 8, panels, 0)

    for copy in firsts:
        copy.wait()
    total = lifted[member]
    for d in range(1, CHILDREN):
        total = total + landed[d - 1]
    summed[...] = total
    mine = pl.ds(pl.multiple_of(member * ROWS, ROWS), ROWS)
    joined[mine, :] = total
    total = rising[leaf]
    for d in range(1, nodes):
        total = total + risen[d - 1]
    rooted[...] = total
    gathered[leaf] = total
    seconds = [
        remote(summed, joined.at[mine], two_send.at[d - 1], two_recv.at[d - 1], {"leaf": peers[d - 1]})
        for d in range(1, CHILDREN)
    ] + [
        remote(rooted, gathered.at[leaf], root_send.at[d - 1], root_recv.at[d - 1], {"leaf": others[d - 1]})
        for d in range(1, nodes)
    ]
    for copy in seconds:
        copy.start()
    up.wait()
    down.wait()

    def halo_features(e, carry):
        s = halo[e]
        there = jnp.where(e < 2, slab > 0, slab < slabs - 1).astype(f32)
        features[CHILDREN + e] = source_features(s[0:1], s[1:2], s[2:3], s[3:4] * there).T.astype(bf16)
        return carry

    lax.fori_loop(0, 4, halo_features, 0)
    lax.fori_loop(0, CHILDREN, near, 0)
    for copy in seconds:
        copy.wait()
    reduced[0] = joined[...]
    for c in range(nodes):
        reduced[1, c * part : (c + 1) * part, :] = gathered[c]


def finish(
    uppers, reduced, partial, features, positions, counts, neighbours,
    leaf_out, node_out, group_out, root_out, near_out, leaves, grams, tops, done,
):
    points = lax.broadcasted_iota(jnp.int32, (1, PTS), 1)
    for l in range(CHILDREN):
        leaves[l] = uppers[l].T
    copy = pltpu.make_async_copy(leaves, leaf_out, done)
    copy.start()
    node_out[...] = uppers[CHILDREN].T
    grams[...] = reduced[...]

    def step(l, carry):
        row = pl.ds(l, 1)
        total = partial[l]
        if EARLY < NB:
            form = target_features(positions[0, row, :], positions[1, row, :], positions[2, row, :])
            total = total + field_of(form, features, [neighbours[k, l] for k in range(EARLY, NB)])
        factor_panel(grams, tops, range(2), l, 16)
        near_out[row, :] = jnp.where(points < counts[0, l], 0.03 * jnp.sum(total, axis=0, keepdims=True), 0.0)
        return carry

    lax.fori_loop(0, CHILDREN, step, 0)
    group_out[...] = tops[0].T
    root_out[...] = tops[1].T
    copy.wait()


def body(
    leaf_basis,
    point_counts,
    leaf_transfer,
    node_transfer,
    group_transfer,
    positions,
    moments,
    send_tiles,
    neighbours,
):
    nodes = lax.axis_size("leaf")
    slabs = lax.axis_size("slab")
    vmem = pl.BlockSpec(memory_space=pltpu.VMEM)
    smem = pl.BlockSpec(memory_space=pltpu.SMEM)
    square = jax.ShapeDtypeStruct((RANK, RANK), f32)
    dma = pltpu.SemaphoreType.DMA
    part = RANK // nodes
    places = jnp.transpose(positions[0], (1, 0, 2))
    links = jnp.transpose(neighbours[0])
    uppers, reduced, partial, features = pl.pallas_call(
        functools.partial(kernel, slabs, nodes),
        out_shape=(
            jax.ShapeDtypeStruct((CHILDREN + 1, RANK, RANK), f32),
            jax.ShapeDtypeStruct((2, RANK, RANK), f32),
            jax.ShapeDtypeStruct((CHILDREN, 8, PTS), f32),
            jax.ShapeDtypeStruct((CHILDREN + 4, PTS, 2 * SPLIT), bf16),
        ),
        in_specs=[vmem] * 6 + [smem] * 3,
        out_specs=(vmem,) * 4,
        scratch_shapes=[
            pltpu.VMEM((CHILDREN, 4, PTS), f32),
            pltpu.VMEM((4, 4, PTS), f32),
            pltpu.VMEM((4, 4, PTS), f32),
            pltpu.VMEM((CHILDREN + 1, RANK, RANK), f32),
            pltpu.VMEM((CHILDREN, ROWS, RANK), f32),
            pltpu.VMEM((CHILDREN - 1, ROWS, RANK), f32),
            pltpu.VMEM((ROWS, RANK), f32),
            pltpu.VMEM((nodes, part, RANK), f32),
            pltpu.VMEM((nodes - 1, part, RANK), f32),
            pltpu.VMEM((part, RANK), f32),
            pltpu.VMEM((nodes, part, RANK), f32),
            pltpu.VMEM((RANK, RANK), f32),
            dma((2,)),
            dma((2,)),
            dma((CHILDREN - 1,)),
            dma((CHILDREN - 1,)),
            dma((CHILDREN - 1,)),
            dma((CHILDREN - 1,)),
            dma((nodes - 1,)),
            dma((nodes - 1,)),
            dma((nodes - 1,)),
            dma((nodes - 1,)),
        ],
        compiler_params=pltpu.CompilerParams(
            collective_id=0, has_side_effects=True, vmem_limit_bytes=24 * 1024 * 1024
        ),
        name="upsweep",
    )(
        leaf_basis[0],
        leaf_transfer[0],
        node_transfer[0, 0],
        group_transfer[0],
        places,
        moments[0],
        point_counts,
        send_tiles,
        links,
    )
    leaf, node, group, root, near = pl.pallas_call(
        finish,
        out_shape=(
            jax.ShapeDtypeStruct((CHILDREN, RANK, RANK), f32),
            square,
            square,
            square,
            jax.ShapeDtypeStruct((CHILDREN, PTS), f32),
        ),
        in_specs=[vmem] * 5 + [smem] * 2,
        out_specs=(pl.BlockSpec(memory_space=pl.ANY),) + (vmem,) * 4,
        scratch_shapes=[
            pltpu.VMEM((CHILDREN, RANK, RANK), f32),
            pltpu.VMEM((2, RANK, RANK), f32),
            pltpu.VMEM((2, RANK, RANK), f32),
            dma,
        ],
        compiler_params=pltpu.CompilerParams(vmem_limit_bytes=24 * 1024 * 1024),
        name="finish",
    )(uppers, reduced, partial, features, places, point_counts, links)
    return leaf[None], node[None, None], group[None, None], root[None, None], near[None]


def solution(mesh):
    in_specs = (
        P("slab", "leaf", None, None),
        P("slab", "leaf"),
        P("slab", "leaf", None, None),
        P("slab", "leaf", None, None),
        P("slab", None, None, None),
        P("slab", "leaf", None, None),
        P("slab", "leaf", None),
        P("slab", "leaf"),
        P("slab", "leaf", None),
    )
    out_specs = (
        P("slab", "leaf", None, None),
        P("slab", "leaf", None, None),
        P("slab", "leaf", None, None),
        P("slab", "leaf", None, None),
        P("slab", "leaf", None),
    )
    return jax.shard_map(body, mesh=mesh, in_specs=in_specs, out_specs=out_specs, check_vma=False)
```

```python
import functools

import jax
import jax.numpy as jnp
from jax import lax
from jax.experimental import pallas as pl
from jax.experimental.pallas import tpu as pltpu
from jax.sharding import PartitionSpec as P

RANK = 128
PTS = 512
CHILDREN = 8
NB = 4
ROWS = 16
AHEAD = 2
EARLY = 3
SPLIT = 48
MESH = pltpu.MESH if hasattr(pltpu, "MESH") else pl.DeviceIdType.MESH

f32 = jnp.float32
bf16 = jnp.bfloat16
highest = lax.Precision.HIGHEST
over_rows = (((0,), (0,)), ((), ()))


def split3(x):
    high = x.astype(bf16)
    rest = x - high.astype(f32)
    middle = rest.astype(bf16)
    return high, middle, (rest - middle.astype(f32)).astype(bf16)


def factor_panel(grams, uppers, mats, k, size):
    groups = size // 8
    sub = lax.broadcasted_iota(jnp.int32, (8, RANK), 0)
    lane = lax.broadcasted_iota(jnp.int32, (8, RANK), 1)
    start = pl.multiple_of(k * size, size)
    count = len(mats)

    def spread(x, s):
        return jnp.broadcast_to(x[s : s + 1, :], (8, RANK))

    rows = [[grams[m, pl.ds(pl.multiple_of(start + 8 * g, 8), 8), :] for g in range(groups)] for m in mats]
    columns = [
        [
            [
                jnp.take_along_axis(rows[i][g], jnp.full((8, RANK), start + j, jnp.int32), axis=1)
                if g >= j // 8
                else None
                for g in range(groups)
            ]
            for j in range(size)
        ]
        for i in range(count)
    ]
    upper = [[None] * groups for _ in mats]
    for r in range(size):
        gr, sr = divmod(r, 8)
        for i in range(count):
            pivot = spread(columns[i][r][gr], sr)
            inverse = 1.0 / pivot
            row = spread(rows[i][gr], sr)
            scaled = row * lax.rsqrt(pivot)
            upper[i][gr] = scaled if sr == 0 else jnp.where(sub >= sr, scaled, upper[i][gr])
            weights = {}
            for g in range(gr, groups):
                if g == gr and sr == 7:
                    continue
                weight = columns[i][r][g] * inverse
                weights[g] = jnp.where(sub > sr, weight, 0.0) if g == gr else weight
            for j in range(r + 1, size):
                entry = spread(columns[i][r][j // 8], j % 8)
                for g in range(max(gr, j // 8), groups):
                    if g in weights:
                        columns[i][j][g] = columns[i][j][g] - weights[g] * entry
            for g in weights:
                rows[i][g] = rows[i][g] - weights[g] * row
    for i, m in enumerate(mats):
        kept = [jnp.where(lane >= sub + (start + 8 * g), upper[i][g], 0.0) for g in range(groups)]
        panel = jnp.concatenate(kept, axis=0) if groups > 1 else kept[0]
        uppers[m, pl.ds(start, size), :] = panel
        high, middle, low = split3(panel)
        left = jnp.concatenate([high, high, high, middle, middle, low], axis=0)
        right = jnp.concatenate([high, middle, low, high, middle, high], axis=0)
        grams[m] = grams[m] - lax.dot_general(left, right, over_rows, preferred_element_type=f32)


def stacked(values):
    rows = lax.broadcasted_iota(jnp.int32, (8, PTS), 0)
    out = jnp.zeros((8, PTS), f32)
    for i, value in enumerate(values):
        out = jnp.where(rows == i, jnp.broadcast_to(value, (8, PTS)), out)
    return out


def source_features(x, y, z, q):
    x, y, z = x - 1.0, y - 1.0, z - 1.0
    flat, high2 = x * x + y * y, z * z
    one, none = jnp.ones_like(x), jnp.zeros_like(x)
    first = stacked([-2.0 * x, -2.0 * y, -2.0 * z, one, none, flat + high2 + 0.25])
    second = stacked([-2.0 * x * q, -2.0 * y * q, 4.0 * z * q, none, q, q * (flat - 2.0 * high2 + 0.25)])
    out = []
    for form in (first, second):
        high, middle, low = [piece.astype(f32) for piece in split3(form)]
        out += [high, middle, low, high, middle, high]
    return jnp.concatenate(out, axis=0)


def target_features(x, y, z):
    x, y, z = x - 1.0, y - 1.0, z - 1.0
    flat, high2 = x * x + y * y, z * z
    form = stacked([x, y, z, flat + high2, flat - 2.0 * high2, jnp.ones_like(x)])
    high, middle, low = [piece.astype(f32) for piece in split3(form)]
    return jnp.concatenate([high, high, high, middle, middle, low], axis=0).astype(bf16)


def field_of(targets, features, picks, width=256, depth=64):
    none = jnp.zeros((SPLIT, width), bf16)
    out = []
    for j in range(PTS // width):
        form = targets[:, j * width : (j + 1) * width]
        for_radius = jnp.concatenate([form, none], axis=0)
        for_weight = jnp.concatenate([none, form], axis=0)
        total = jnp.zeros((8, width), f32)
        for pick in picks:
            for c in range(PTS // depth):
                block = features[pick, c * depth : (c + 1) * depth, :]
                radius = jnp.dot(block, for_radius, preferred_element_type=f32)
                weight = jnp.dot(block, for_weight, preferred_element_type=f32)
                root = lax.rsqrt(radius)
                square = root * root
                value = (weight * root) * (square * square)
                total = total + jnp.sum(value.reshape(depth // 8, 8, width), axis=0)
        out.append(total)
    return jnp.concatenate(out, axis=1)


def kernel(
    slabs,
    nodes,
    basis_hbm,
    leaf_transfer_hbm,
    node_transfer_hbm,
    group_transfer_hbm,
    positions_hbm,
    moments_hbm,
    counts_hbm,
    tiles_hbm,
    neighbours_hbm,
    uppers,
    reduced,
    partial,
    features,
    basis,
    leaf_transfer,
    node_transfer,
    group_transfer,
    positions,
    moments,
    counts,
    tiles,
    neighbours,
    basis_done,
    loaded,
    own,
    faces,
    halo,
    grams,
    lifted,
    landed,
    summed,
    rising,
    risen,
    rooted,
    gathered,
    joined,
    face_send,
    face_recv,
    one_send,
    one_recv,
    two_send,
    two_recv,
    rise_send,
    rise_recv,
    root_send,
    root_recv,
):
    leaf = lax.axis_index("leaf")
    slab = lax.axis_index("slab")
    member, group = leaf % CHILDREN, leaf // CHILDREN
    peers = [group * CHILDREN + (member + d) % CHILDREN for d in range(1, CHILDREN)]
    others = [(leaf + d) % nodes for d in range(1, nodes)]
    above, below = (slab + 1) % slabs, (slab + slabs - 1) % slabs
    loads = [
        pltpu.make_async_copy(source, target, loaded.at[i])
        for i, (source, target) in enumerate(
            [
                (counts_hbm, counts),
                (tiles_hbm, tiles),
                (positions_hbm, positions),
                (moments_hbm, moments),
                (neighbours_hbm, neighbours),
                (leaf_transfer_hbm, leaf_transfer),
                (node_transfer_hbm, node_transfer),
                (group_transfer_hbm.at[group], group_transfer),
            ]
        )
    ]
    blocks = [pltpu.make_async_copy(basis_hbm.at[l], basis.at[l], basis_done.at[l]) for l in range(CHILDREN)]
    for copy in loads[:4] + blocks + loads[4:]:
        copy.start()
    barrier = pltpu.get_barrier_semaphore()
    for other in others:
        pl.semaphore_signal(barrier, inc=1, device_id={"leaf": other}, device_id_type=MESH)
    for other in (above, below):
        pl.semaphore_signal(barrier, inc=1, device_id={"slab": other}, device_id_type=MESH)

    points = lax.broadcasted_iota(jnp.int32, (1, PTS), 1)
    for copy in loads[:4]:
        copy.wait()
    for l in range(CHILDREN):
        for axis in range(3):
            own[l, axis : axis + 1, :] = positions[axis, l : l + 1, :]
        own[l, 3:4, :] = moments[l : l + 1, :] * (points < counts[0, l]).astype(f32)
    for f in range(4):
        faces[f] = own[tiles[0, f]]

    slots = lax.broadcasted_iota(jnp.int32, (PTS, RANK), 0)
    inner = []
    for copy in blocks + loads[4:]:
        copy.wait()
    for l in range(CHILDREN):
        live = jnp.where(slots < counts[0, l], basis[l].astype(f32), 0.0).astype(bf16)
        gram = lax.dot_general(live, live, over_rows, preferred_element_type=f32)
        grams[l] = gram
        inner.append(jnp.dot(gram, leaf_transfer[l], precision=highest, preferred_element_type=f32))
    every = leaf_transfer[...].reshape(CHILDREN * RANK, RANK)
    node = lax.dot_general(every, jnp.concatenate(inner, axis=0), over_rows, precision=highest, preferred_element_type=f32)
    grams[CHILDREN] = node

    def congruent(transfer, gram):
        product = jnp.dot(gram, transfer, precision=highest, preferred_element_type=f32)
        return lax.dot_general(transfer, product, over_rows, precision=highest, preferred_element_type=f32)

    to_group = congruent(node_transfer[...], node)
    to_root = congruent(group_transfer[...], to_group)
    part = RANK // nodes
    for c in range(CHILDREN):
        lifted[c] = to_group[c * ROWS : (c + 1) * ROWS, :]
    for c in range(nodes):
        rising[c] = to_root[c * part : (c + 1) * part, :]

    def own_features(l, carry):
        s = own[l]
        features[l] = source_features(s[0:1], s[1:2], s[2:3], s[3:4]).T.astype(bf16)
        return carry

    lax.fori_loop(0, CHILDREN, own_features, 0)

    def panels(k, carry):
        factor_panel(grams, uppers, range(CHILDREN + 1), k, 8)
        return carry

    def near(l, carry):
        s = own[l]
        partial[l] = field_of(
            target_features(s[0:1], s[1:2], s[2:3]), features, [neighbours[k, l] for k in range(EARLY)]
        )
        return carry

    lax.fori_loop(0, AHEAD, panels, 0)

    pl.semaphore_wait(barrier, len(others) + 2)

    def remote(source, target, send, recv, where):
        return pltpu.make_async_remote_copy(
            src_ref=source, dst_ref=target, send_sem=send, recv_sem=recv, device_id=where, device_id_type=MESH
        )

    up = remote(faces.at[pl.ds(2, 2)], halo.at[pl.ds(0, 2)], face_send.at[0], face_recv.at[0], {"slab": above})
    down = remote(faces.at[pl.ds(0, 2)], halo.at[pl.ds(2, 2)], face_send.at[1], face_recv.at[1], {"slab": below})
    up.start()
    down.start()
    firsts = [
        remote(
            lifted.at[(member + d) % CHILDREN],
            landed.at[d - 1],
            one_send.at[d - 1],
            one_recv.at[d - 1],
            {"leaf": peers[d - 1]},
        )
        for d in range(1, CHILDREN)
    ] + [
        remote(
            rising.at[(leaf + d) % nodes],
            risen.at[d - 1],
            rise_send.at[d - 1],
            rise_recv.at[d - 1],
            {"leaf": others[d - 1]},
        )
        for d in range(1, nodes)
    ]
    for copy in firsts:
        copy.start()

    lax.fori_loop(AHEAD, RANK // 8, panels, 0)

    for copy in firsts:
        copy.wait()
    total = lifted[member]
    for d in range(1, CHILDREN):
        total = total + landed[d - 1]
    summed[...] = total
    mine = pl.ds(pl.multiple_of(member * ROWS, ROWS), ROWS)
    joined[mine, :] = total
    total = rising[leaf]
    for d in range(1, nodes):
        total = total + risen[d - 1]
    rooted[...] = total
    gathered[leaf] = total
    seconds = [
        remote(summed, joined.at[mine], two_send.at[d - 1], two_recv.at[d - 1], {"leaf": peers[d - 1]})
        for d in range(1, CHILDREN)
    ] + [
        remote(rooted, gathered.at[leaf], root_send.at[d - 1], root_recv.at[d - 1], {"leaf": others[d - 1]})
        for d in range(1, nodes)
    ]
    for copy in seconds:
        copy.start()
    up.wait()
    down.wait()

    def halo_features(e, carry):
        s = halo[e]
        there = jnp.where(e < 2, slab > 0, slab < slabs - 1).astype(f32)
        features[CHILDREN + e] = source_features(s[0:1], s[1:2], s[2:3], s[3:4] * there).T.astype(bf16)
        return carry

    lax.fori_loop(0, 4, halo_features, 0)
    lax.fori_loop(0, CHILDREN, near, 0)
    for copy in seconds:
        copy.wait()
    reduced[0] = joined[...]
    for c in range(nodes):
        reduced[1, c * part : (c + 1) * part, :] = gathered[c]


def finish(
    uppers,
    reduced,
    partial,
    features,
    positions_hbm,
    counts_hbm,
    neighbours_hbm,
    leaf_out,
    node_out,
    group_out,
    root_out,
    near_out,
    positions,
    counts,
    neighbours,
    loaded,
    leaves,
    grams,
    tops,
    done,
):
    loads = [
        pltpu.make_async_copy(positions_hbm, positions, loaded.at[0]),
        pltpu.make_async_copy(counts_hbm, counts, loaded.at[1]),
        pltpu.make_async_copy(neighbours_hbm, neighbours, loaded.at[2]),
    ]
    for copy in loads:
        copy.start()
    points = lax.broadcasted_iota(jnp.int32, (1, PTS), 1)
    for l in range(CHILDREN):
        leaves[l] = uppers[l].T
    copy = pltpu.make_async_copy(leaves, leaf_out, done)
    copy.start()
    node_out[...] = uppers[CHILDREN].T
    grams[...] = reduced[...]
    for load in loads:
        load.wait()

    def step(l, carry):
        row = pl.ds(l, 1)
        total = partial[l]
        if EARLY < NB:
            form = target_features(positions[0, row, :], positions[1, row, :], positions[2, row, :])
            total = total + field_of(form, features, [neighbours[k, l] for k in range(EARLY, NB)])
        factor_panel(grams, tops, range(2), l, 16)
        near_out[row, :] = jnp.where(points < counts[0, l], 0.03 * jnp.sum(total, axis=0, keepdims=True), 0.0)
        return carry

    lax.fori_loop(0, CHILDREN, step, 0)
    group_out[...] = tops[0].T
    root_out[...] = tops[1].T
    copy.wait()


def pin(array):
    return pltpu.with_memory_space_constraint(array, pltpu.HBM)


def body(
    leaf_basis,
    point_counts,
    leaf_transfer,
    node_transfer,
    group_transfer,
    positions,
    moments,
    send_tiles,
    neighbours,
):
    nodes = lax.axis_size("leaf")
    slabs = lax.axis_size("slab")
    vmem = pl.BlockSpec(memory_space=pltpu.VMEM)
    hbm = pl.BlockSpec(memory_space=pltpu.HBM)
    square = jax.ShapeDtypeStruct((RANK, RANK), f32)
    dma = pltpu.SemaphoreType.DMA
    part = RANK // nodes
    places = jnp.transpose(positions[0], (1, 0, 2))
    links = jnp.transpose(neighbours[0])
    uppers, reduced, partial, features = pl.pallas_call(
        functools.partial(kernel, slabs, nodes),
        out_shape=(
            jax.ShapeDtypeStruct((CHILDREN + 1, RANK, RANK), f32),
            jax.ShapeDtypeStruct((2, RANK, RANK), f32),
            jax.ShapeDtypeStruct((CHILDREN, 8, PTS), f32),
            jax.ShapeDtypeStruct((CHILDREN + 4, PTS, 2 * SPLIT), bf16),
        ),
        in_specs=[hbm] * 9,
        out_specs=(vmem,) * 4,
        scratch_shapes=[
            pltpu.VMEM((CHILDREN, PTS, RANK), bf16),
            pltpu.VMEM((CHILDREN, RANK, RANK), f32),
            pltpu.VMEM((RANK, RANK), f32),
            pltpu.VMEM((RANK, RANK), f32),
            pltpu.VMEM((3, CHILDREN, PTS), f32),
            pltpu.VMEM((CHILDREN, PTS), f32),
            pltpu.SMEM((1, CHILDREN), jnp.int32),
            pltpu.SMEM((1, 4), jnp.int32),
            pltpu.SMEM((NB, CHILDREN), jnp.int32),
            dma((CHILDREN,)),
            dma((8,)),
            pltpu.VMEM((CHILDREN, 4, PTS), f32),
            pltpu.VMEM((4, 4, PTS), f32),
            pltpu.VMEM((4, 4, PTS), f32),
            pltpu.VMEM((CHILDREN + 1, RANK, RANK), f32),
            pltpu.VMEM((CHILDREN, ROWS, RANK), f32),
            pltpu.VMEM((CHILDREN - 1, ROWS, RANK), f32),
            pltpu.VMEM((ROWS, RANK), f32),
            pltpu.VMEM((nodes, part, RANK), f32),
            pltpu.VMEM((nodes - 1, part, RANK), f32),
            pltpu.VMEM((part, RANK), f32),
            pltpu.VMEM((nodes, part, RANK), f32),
            pltpu.VMEM((RANK, RANK), f32),
            dma((2,)),
            dma((2,)),
            dma((CHILDREN - 1,)),
            dma((CHILDREN - 1,)),
            dma((CHILDREN - 1,)),
            dma((CHILDREN - 1,)),
            dma((nodes - 1,)),
            dma((nodes - 1,)),
            dma((nodes - 1,)),
            dma((nodes - 1,)),
        ],
        compiler_params=pltpu.CompilerParams(
            collective_id=0, has_side_effects=True, vmem_limit_bytes=24 * 1024 * 1024
        ),
        name="upsweep",
    )(
        pin(leaf_basis[0]),
        pin(leaf_transfer[0]),
        pin(node_transfer[0, 0]),
        pin(group_transfer[0]),
        pin(places),
        pin(moments[0]),
        pin(point_counts),
        pin(send_tiles),
        pin(links),
    )
    leaf, node, group, root, near = pl.pallas_call(
        finish,
        out_shape=(
            jax.ShapeDtypeStruct((CHILDREN, RANK, RANK), f32),
            square,
            square,
            square,
            jax.ShapeDtypeStruct((CHILDREN, PTS), f32),
        ),
        in_specs=[vmem] * 4 + [hbm] * 3,
        out_specs=(hbm,) + (vmem,) * 4,
        scratch_shapes=[
            pltpu.VMEM((3, CHILDREN, PTS), f32),
            pltpu.SMEM((1, CHILDREN), jnp.int32),
            pltpu.SMEM((NB, CHILDREN), jnp.int32),
            dma((3,)),
            pltpu.VMEM((CHILDREN, RANK, RANK), f32),
            pltpu.VMEM((2, RANK, RANK), f32),
            pltpu.VMEM((2, RANK, RANK), f32),
            dma,
        ],
        compiler_params=pltpu.CompilerParams(vmem_limit_bytes=24 * 1024 * 1024),
        name="finish",
    )(uppers, reduced, partial, features, pin(places), pin(point_counts), pin(links))
    return leaf[None], node[None, None], group[None, None], root[None, None], near[None]


def solution(mesh):
    in_specs = (
        P("slab", "leaf", None, None),
        P("slab", "leaf"),
        P("slab", "leaf", None, None),
        P("slab", "leaf", None, None),
        P("slab", None, None, None),
        P("slab", "leaf", None, None),
        P("slab", "leaf", None),
        P("slab", "leaf"),
        P("slab", "leaf", None),
    )
    out_specs = (
        P("slab", "leaf", None, None),
        P("slab", "leaf", None, None),
        P("slab", "leaf", None, None),
        P("slab", "leaf", None, None),
        P("slab", "leaf", None),
    )
    return jax.shard_map(body, mesh=mesh, in_specs=in_specs, out_specs=out_specs, check_vma=False)
```

```python
import functools

import jax
import jax.numpy as jnp
from jax import lax
from jax.experimental import pallas as pl
from jax.experimental.pallas import tpu as pltpu
from jax.sharding import PartitionSpec as P

RANK = 128
PTS = 512
CHILDREN = 8
NB = 4
ROWS = 16
BEFORE = 1
AHEAD = 4
EARLY = 3
SPLIT = 48
MESH = pltpu.MESH if hasattr(pltpu, "MESH") else pl.DeviceIdType.MESH

f32 = jnp.float32
bf16 = jnp.bfloat16
highest = lax.Precision.HIGHEST
over_rows = (((0,), (0,)), ((), ()))


def split3(x):
    high = x.astype(bf16)
    rest = x - high.astype(f32)
    middle = rest.astype(bf16)
    return high, middle, (rest - middle.astype(f32)).astype(bf16)


def factor_panel(grams, uppers, mats, k, size):
    groups = size // 8
    sub = lax.broadcasted_iota(jnp.int32, (8, RANK), 0)
    lane = lax.broadcasted_iota(jnp.int32, (8, RANK), 1)
    start = pl.multiple_of(k * size, size)
    count = len(mats)

    def spread(x, s):
        return jnp.broadcast_to(x[s : s + 1, :], (8, RANK))

    rows = [[grams[m, pl.ds(pl.multiple_of(start + 8 * g, 8), 8), :] for g in range(groups)] for m in mats]
    columns = [
        [
            [
                jnp.take_along_axis(rows[i][g], jnp.full((8, RANK), start + j, jnp.int32), axis=1)
                if g >= j // 8
                else None
                for g in range(groups)
            ]
            for j in range(size)
        ]
        for i in range(count)
    ]
    upper = [[None] * groups for _ in mats]
    for r in range(size):
        gr, sr = divmod(r, 8)
        for i in range(count):
            pivot = spread(columns[i][r][gr], sr)
            inverse = 1.0 / pivot
            row = spread(rows[i][gr], sr)
            scaled = row * lax.rsqrt(pivot)
            upper[i][gr] = scaled if sr == 0 else jnp.where(sub >= sr, scaled, upper[i][gr])
            weights = {}
            for g in range(gr, groups):
                if g == gr and sr == 7:
                    continue
                weight = columns[i][r][g] * inverse
                weights[g] = jnp.where(sub > sr, weight, 0.0) if g == gr else weight
            for j in range(r + 1, size):
                entry = spread(columns[i][r][j // 8], j % 8)
                for g in range(max(gr, j // 8), groups):
                    if g in weights:
                        columns[i][j][g] = columns[i][j][g] - weights[g] * entry
            for g in weights:
                rows[i][g] = rows[i][g] - weights[g] * row
    for i, m in enumerate(mats):
        kept = [jnp.where(lane >= sub + (start + 8 * g), upper[i][g], 0.0) for g in range(groups)]
        panel = jnp.concatenate(kept, axis=0) if groups > 1 else kept[0]
        uppers[m, pl.ds(start, size), :] = panel
        high, middle, low = split3(panel)
        left = jnp.concatenate([high, high, high, middle, middle, low], axis=0)
        right = jnp.concatenate([high, middle, low, high, middle, high], axis=0)
        grams[m] = grams[m] - lax.dot_general(left, right, over_rows, preferred_element_type=f32)


def stacked(values):
    rows = lax.broadcasted_iota(jnp.int32, (8, PTS), 0)
    out = jnp.zeros((8, PTS), f32)
    for i, value in enumerate(values):
        out = jnp.where(rows == i, jnp.broadcast_to(value, (8, PTS)), out)
    return out


def source_features(x, y, z, q):
    x, y, z = x - 1.0, y - 1.0, z - 1.0
    flat, high2 = x * x + y * y, z * z
    one, none = jnp.ones_like(x), jnp.zeros_like(x)
    first = stacked([-2.0 * x, -2.0 * y, -2.0 * z, one, none, flat + high2 + 0.25])
    second = stacked([-2.0 * x * q, -2.0 * y * q, 4.0 * z * q, none, q, q * (flat - 2.0 * high2 + 0.25)])
    out = []
    for form in (first, second):
        high, middle, low = [piece.astype(f32) for piece in split3(form)]
        out += [high, middle, low, high, middle, high]
    return jnp.concatenate(out, axis=0)


def target_features(x, y, z):
    x, y, z = x - 1.0, y - 1.0, z - 1.0
    flat, high2 = x * x + y * y, z * z
    form = stacked([x, y, z, flat + high2, flat - 2.0 * high2, jnp.ones_like(x)])
    high, middle, low = [piece.astype(f32) for piece in split3(form)]
    return jnp.concatenate([high, high, high, middle, middle, low], axis=0).astype(bf16)


def field_of(targets, features, picks, width=256, depth=64):
    none = jnp.zeros((SPLIT, width), bf16)
    out = []
    for j in range(PTS // width):
        form = targets[:, j * width : (j + 1) * width]
        for_radius = jnp.concatenate([form, none], axis=0)
        for_weight = jnp.concatenate([none, form], axis=0)
        total = jnp.zeros((8, width), f32)
        for pick in picks:
            for c in range(PTS // depth):
                block = features[pick, c * depth : (c + 1) * depth, :]
                radius = jnp.dot(block, for_radius, preferred_element_type=f32)
                weight = jnp.dot(block, for_weight, preferred_element_type=f32)
                root = lax.rsqrt(radius)
                square = root * root
                value = (weight * root) * (square * square)
                total = total + jnp.sum(value.reshape(depth // 8, 8, width), axis=0)
        out.append(total)
    return jnp.concatenate(out, axis=1)


def kernel(
    slabs,
    nodes,
    basis_hbm,
    leaf_transfer_hbm,
    node_transfer_hbm,
    group_transfer_hbm,
    positions_hbm,
    moments_hbm,
    counts_hbm,
    tiles_hbm,
    neighbours_hbm,
    uppers,
    reduced,
    partial,
    features,
    basis,
    leaf_transfer,
    node_transfer,
    group_transfer,
    positions,
    moments,
    counts,
    tiles,
    neighbours,
    basis_done,
    loaded,
    own,
    faces,
    halo,
    grams,
    lifted,
    landed,
    summed,
    rising,
    risen,
    rooted,
    gathered,
    joined,
    face_send,
    face_recv,
    one_send,
    one_recv,
    two_send,
    two_recv,
    rise_send,
    rise_recv,
    root_send,
    root_recv,
):
    leaf = lax.axis_index("leaf")
    slab = lax.axis_index("slab")
    member, group = leaf % CHILDREN, leaf // CHILDREN
    peers = [group * CHILDREN + (member + d) % CHILDREN for d in range(1, CHILDREN)]
    others = [(leaf + d) % nodes for d in range(1, nodes)]
    above, below = (slab + 1) % slabs, (slab + slabs - 1) % slabs
    loads = [
        pltpu.make_async_copy(source, target, loaded.at[i])
        for i, (source, target) in enumerate(
            [
                (counts_hbm, counts),
                (tiles_hbm, tiles),
                (positions_hbm, positions),
                (moments_hbm, moments),
                (neighbours_hbm, neighbours),
                (leaf_transfer_hbm, leaf_transfer),
                (node_transfer_hbm, node_transfer),
                (group_transfer_hbm.at[group], group_transfer),
            ]
        )
    ]
    blocks = [pltpu.make_async_copy(basis_hbm.at[l], basis.at[l], basis_done.at[l]) for l in range(CHILDREN)]
    for copy in loads[:4] + blocks + loads[4:]:
        copy.start()
    barrier = pltpu.get_barrier_semaphore()
    for other in others:
        pl.semaphore_signal(barrier, inc=1, device_id={"leaf": other}, device_id_type=MESH)
    for other in (above, below):
        pl.semaphore_signal(barrier, inc=1, device_id={"slab": other}, device_id_type=MESH)

    points = lax.broadcasted_iota(jnp.int32, (1, PTS), 1)
    for copy in loads[:4]:
        copy.wait()
    for l in range(CHILDREN):
        for axis in range(3):
            own[l, axis : axis + 1, :] = positions[axis, l : l + 1, :]
        own[l, 3:4, :] = moments[l : l + 1, :] * (points < counts[0, l]).astype(f32)
    for f in range(4):
        faces[f] = own[tiles[0, f]]

    slots = lax.broadcasted_iota(jnp.int32, (PTS, RANK), 0)
    inner = []
    for copy in blocks + loads[4:]:
        copy.wait()
    for l in range(CHILDREN):
        live = jnp.where(slots < counts[0, l], basis[l].astype(f32), 0.0).astype(bf16)
        gram = lax.dot_general(live, live, over_rows, preferred_element_type=f32)
        grams[l] = gram
        inner.append(jnp.dot(gram, leaf_transfer[l], precision=highest, preferred_element_type=f32))
    to_parent = node_transfer[...]
    to_top = jnp.dot(to_parent, group_transfer[...], precision=highest, preferred_element_type=f32)
    every = leaf_transfer[...].reshape(CHILDREN * RANK, RANK)
    node = lax.dot_general(every, jnp.concatenate(inner, axis=0), over_rows, precision=highest, preferred_element_type=f32)
    grams[CHILDREN] = node

    def product(left, right):
        return jnp.dot(left, right, precision=highest, preferred_element_type=f32)

    def from_left(transfer, right):
        return lax.dot_general(transfer, right, over_rows, precision=highest, preferred_element_type=f32)

    both = product(node, jnp.concatenate([to_parent, to_top], axis=1))
    to_group = from_left(to_parent, both[:, :RANK])
    to_root = from_left(to_top, both[:, RANK:])
    part = RANK // nodes
    for c in range(CHILDREN):
        lifted[c] = to_group[c * ROWS : (c + 1) * ROWS, :]
    for c in range(nodes):
        rising[c] = to_root[c * part : (c + 1) * part, :]

    def own_features(l, carry):
        s = own[l]
        features[l] = source_features(s[0:1], s[1:2], s[2:3], s[3:4]).T.astype(bf16)
        return carry

    lax.fori_loop(0, CHILDREN, own_features, 0)

    def panels(k, carry):
        factor_panel(grams, uppers, range(CHILDREN + 1), k, 8)
        return carry

    def near(l, carry):
        s = own[l]
        partial[l] = field_of(
            target_features(s[0:1], s[1:2], s[2:3]), features, [neighbours[k, l] for k in range(EARLY)]
        )
        return carry

    lax.fori_loop(0, AHEAD, panels, 0)

    pl.semaphore_wait(barrier, len(others) + 2)

    def remote(source, target, send, recv, where):
        return pltpu.make_async_remote_copy(
            src_ref=source, dst_ref=target, send_sem=send, recv_sem=recv, device_id=where, device_id_type=MESH
        )

    up = remote(faces.at[pl.ds(2, 2)], halo.at[pl.ds(0, 2)], face_send.at[0], face_recv.at[0], {"slab": above})
    down = remote(faces.at[pl.ds(0, 2)], halo.at[pl.ds(2, 2)], face_send.at[1], face_recv.at[1], {"slab": below})
    up.start()
    down.start()
    firsts = [
        remote(
            lifted.at[(member + d) % CHILDREN],
            landed.at[d - 1],
            one_send.at[d - 1],
            one_recv.at[d - 1],
            {"leaf": peers[d - 1]},
        )
        for d in range(1, CHILDREN)
    ] + [
        remote(
            rising.at[(leaf + d) % nodes],
            risen.at[d - 1],
            rise_send.at[d - 1],
            rise_recv.at[d - 1],
            {"leaf": others[d - 1]},
        )
        for d in range(1, nodes)
    ]
    for copy in firsts:
        copy.start()

    lax.fori_loop(AHEAD, RANK // 8, panels, 0)

    up.wait()
    down.wait()

    def halo_features(e, carry):
        s = halo[e]
        there = jnp.where(e < 2, slab > 0, slab < slabs - 1).astype(f32)
        features[CHILDREN + e] = source_features(s[0:1], s[1:2], s[2:3], s[3:4] * there).T.astype(bf16)
        return carry

    lax.fori_loop(0, 4, halo_features, 0)
    lax.fori_loop(0, BEFORE, near, 0)

    for copy in firsts:
        copy.wait()
    total = lifted[member]
    for d in range(1, CHILDREN):
        total = total + landed[d - 1]
    summed[...] = total
    mine = pl.ds(pl.multiple_of(member * ROWS, ROWS), ROWS)
    joined[mine, :] = total
    total = rising[leaf]
    for d in range(1, nodes):
        total = total + risen[d - 1]
    rooted[...] = total
    gathered[leaf] = total
    seconds = [
        remote(summed, joined.at[mine], two_send.at[d - 1], two_recv.at[d - 1], {"leaf": peers[d - 1]})
        for d in range(1, CHILDREN)
    ] + [
        remote(rooted, gathered.at[leaf], root_send.at[d - 1], root_recv.at[d - 1], {"leaf": others[d - 1]})
        for d in range(1, nodes)
    ]
    for copy in seconds:
        copy.start()
    lax.fori_loop(BEFORE, CHILDREN, near, 0)
    for copy in seconds:
        copy.wait()
    reduced[0] = joined[...]
    for c in range(nodes):
        reduced[1, c * part : (c + 1) * part, :] = gathered[c]


def finish(
    uppers,
    reduced,
    partial,
    features,
    positions_hbm,
    counts_hbm,
    neighbours_hbm,
    leaf_out,
    node_out,
    group_out,
    root_out,
    near_out,
    positions,
    counts,
    neighbours,
    loaded,
    leaves,
    grams,
    tops,
    done,
):
    loads = [
        pltpu.make_async_copy(positions_hbm, positions, loaded.at[0]),
        pltpu.make_async_copy(counts_hbm, counts, loaded.at[1]),
        pltpu.make_async_copy(neighbours_hbm, neighbours, loaded.at[2]),
    ]
    for copy in loads:
        copy.start()
    points = lax.broadcasted_iota(jnp.int32, (1, PTS), 1)
    for l in range(CHILDREN):
        leaves[l] = uppers[l].T
    copy = pltpu.make_async_copy(leaves, leaf_out, done)
    copy.start()
    node_out[...] = uppers[CHILDREN].T
    grams[...] = reduced[...]
    for load in loads:
        load.wait()

    def step(l, carry):
        row = pl.ds(l, 1)
        total = partial[l]
        if EARLY < NB:
            form = target_features(positions[0, row, :], positions[1, row, :], positions[2, row, :])
            total = total + field_of(form, features, [neighbours[k, l] for k in range(EARLY, NB)])
        factor_panel(grams, tops, range(2), l, 16)
        near_out[row, :] = jnp.where(points < counts[0, l], 0.03 * jnp.sum(total, axis=0, keepdims=True), 0.0)
        return carry

    lax.fori_loop(0, CHILDREN, step, 0)
    group_out[...] = tops[0].T
    root_out[...] = tops[1].T
    copy.wait()


def pin(array):
    return pltpu.with_memory_space_constraint(array, pltpu.HBM)


def body(
    leaf_basis,
    point_counts,
    leaf_transfer,
    node_transfer,
    group_transfer,
    positions,
    moments,
    send_tiles,
    neighbours,
):
    nodes = lax.axis_size("leaf")
    slabs = lax.axis_size("slab")
    vmem = pl.BlockSpec(memory_space=pltpu.VMEM)
    hbm = pl.BlockSpec(memory_space=pltpu.HBM)
    square = jax.ShapeDtypeStruct((RANK, RANK), f32)
    dma = pltpu.SemaphoreType.DMA
    part = RANK // nodes
    places = jnp.transpose(positions[0], (1, 0, 2))
    links = jnp.transpose(neighbours[0])
    uppers, reduced, partial, features = pl.pallas_call(
        functools.partial(kernel, slabs, nodes),
        out_shape=(
            jax.ShapeDtypeStruct((CHILDREN + 1, RANK, RANK), f32),
            jax.ShapeDtypeStruct((2, RANK, RANK), f32),
            jax.ShapeDtypeStruct((CHILDREN, 8, PTS), f32),
            jax.ShapeDtypeStruct((CHILDREN + 4, PTS, 2 * SPLIT), bf16),
        ),
        in_specs=[hbm] * 9,
        out_specs=(vmem,) * 4,
        scratch_shapes=[
            pltpu.VMEM((CHILDREN, PTS, RANK), bf16),
            pltpu.VMEM((CHILDREN, RANK, RANK), f32),
            pltpu.VMEM((RANK, RANK), f32),
            pltpu.VMEM((RANK, RANK), f32),
            pltpu.VMEM((3, CHILDREN, PTS), f32),
            pltpu.VMEM((CHILDREN, PTS), f32),
            pltpu.SMEM((1, CHILDREN), jnp.int32),
            pltpu.SMEM((1, 4), jnp.int32),
            pltpu.SMEM((NB, CHILDREN), jnp.int32),
            dma((CHILDREN,)),
            dma((8,)),
            pltpu.VMEM((CHILDREN, 4, PTS), f32),
            pltpu.VMEM((4, 4, PTS), f32),
            pltpu.VMEM((4, 4, PTS), f32),
            pltpu.VMEM((CHILDREN + 1, RANK, RANK), f32),
            pltpu.VMEM((CHILDREN, ROWS, RANK), f32),
            pltpu.VMEM((CHILDREN - 1, ROWS, RANK), f32),
            pltpu.VMEM((ROWS, RANK), f32),
            pltpu.VMEM((nodes, part, RANK), f32),
            pltpu.VMEM((nodes - 1, part, RANK), f32),
            pltpu.VMEM((part, RANK), f32),
            pltpu.VMEM((nodes, part, RANK), f32),
            pltpu.VMEM((RANK, RANK), f32),
            dma((2,)),
            dma((2,)),
            dma((CHILDREN - 1,)),
            dma((CHILDREN - 1,)),
            dma((CHILDREN - 1,)),
            dma((CHILDREN - 1,)),
            dma((nodes - 1,)),
            dma((nodes - 1,)),
            dma((nodes - 1,)),
            dma((nodes - 1,)),
        ],
        compiler_params=pltpu.CompilerParams(
            collective_id=0, has_side_effects=True, vmem_limit_bytes=24 * 1024 * 1024
        ),
        name="upsweep",
    )(
        pin(leaf_basis[0]),
        pin(leaf_transfer[0]),
        pin(node_transfer[0, 0]),
        pin(group_transfer[0]),
        pin(places),
        pin(moments[0]),
        pin(point_counts),
        pin(send_tiles),
        pin(links),
    )
    leaf, node, group, root, near = pl.pallas_call(
        finish,
        out_shape=(
            jax.ShapeDtypeStruct((CHILDREN, RANK, RANK), f32),
            square,
            square,
            square,
            jax.ShapeDtypeStruct((CHILDREN, PTS), f32),
        ),
        in_specs=[vmem] * 4 + [hbm] * 3,
        out_specs=(hbm,) + (vmem,) * 4,
        scratch_shapes=[
            pltpu.VMEM((3, CHILDREN, PTS), f32),
            pltpu.SMEM((1, CHILDREN), jnp.int32),
            pltpu.SMEM((NB, CHILDREN), jnp.int32),
            dma((3,)),
            pltpu.VMEM((CHILDREN, RANK, RANK), f32),
            pltpu.VMEM((2, RANK, RANK), f32),
            pltpu.VMEM((2, RANK, RANK), f32),
            dma,
        ],
        compiler_params=pltpu.CompilerParams(vmem_limit_bytes=24 * 1024 * 1024),
        name="finish",
    )(uppers, reduced, partial, features, pin(places), pin(point_counts), pin(links))
    return leaf[None], node[None, None], group[None, None], root[None, None], near[None]


def solution(mesh):
    in_specs = (
        P("slab", "leaf", None, None),
        P("slab", "leaf"),
        P("slab", "leaf", None, None),
        P("slab", "leaf", None, None),
        P("slab", None, None, None),
        P("slab", "leaf", None, None),
        P("slab", "leaf", None),
        P("slab", "leaf"),
        P("slab", "leaf", None),
    )
    out_specs = (
        P("slab", "leaf", None, None),
        P("slab", "leaf", None, None),
        P("slab", "leaf", None, None),
        P("slab", "leaf", None, None),
        P("slab", "leaf", None),
    )
    return jax.shard_map(body, mesh=mesh, in_specs=in_specs, out_specs=out_specs, check_vma=False)
```
